256 devices in a mesh: wide: 64 (over x, z_hi, y, core), narrow: 4 (over z_lo).
Axes of the slice: x: 4, y: 4, z: 8 (z_hi: 2, z_lo: 4; z = z_hi * 4 + z_lo), core: 2. Of those that a mesh axis runs over, the one named last changes fastest.
Arguments:
- params: float32 [64, 4, 1024, 512], P('wide', 'narrow'), may hold values from -6 to 6
- public: float32 [64, 4, 1024, 512], P('wide', 'narrow'), may hold values from -6 to 6
- mixed: float32 [64, 4, 1024, 512], P('wide', 'narrow'), may hold values from -6 to 6
- inputs: bfloat16 [64, 4, 256, 1024], P('wide', 'narrow'), may hold values from -6 to 6
- cotangent: bfloat16 [64, 4, 256, 512], P('wide', 'narrow'), may hold values from -1.5 to 1.5
- block_ids: int32 [64, 4, 2, 8], P('wide', 'narrow'), may hold values from 0 to 31, as said below
- block_counts: int32 [64, 4, 2], P('wide', 'narrow'), may hold values from 1 to 8, as said below
Outputs:
- params_out: float32 [64, 4, 1024, 512], P('wide', 'narrow')
- public_out: float32 [64, 4, 1024, 512], P('wide', 'narrow')
- mixed_out: float32 [64, 4, 1024, 512], P('wide', 'narrow')
The draws below stay inside these ranges and needn't reach their ends.
Inputs may be any that keep to these rules, and one draw needn't show every extreme that they name: `block_ids`: each row of 8 entries holds distinct tile numbers; entries past the row's count are unused. `block_counts`: some replica uses all 8 entries in some round in every draw.
All inputs are finite; a program needn't handle non-finite values.
Results may differ from the reference program's by a relative error of at most 0.0003.
Values sent between devices are 32-bit elements; how exact they have to be, the bound alone decides.
No kernel may reach another device: no remote copies, remote signals or barrier semaphores. Data moves between devices by JAX's collectives and lax.ppermute only.
A program may use at most 128 MiB of HBM per device.

```python
import jax
import jax.numpy as jnp

D = 1024
COLS = 512
TILE = 128
KMAX = 8
ROUNDS = 2
TOK_DEV = 256
WIDE_REPL = 64
NARROW_REPL = 4
BLOCKS = 32


def draw_block_ids(key, part):
    total = WIDE_REPL * NARROW_REPL * ROUNDS
    keys = jax.random.split(key, total)
    orders = jax.vmap(lambda single: jax.random.permutation(single, BLOCKS))(keys)
    return orders[:, :KMAX].astype(jnp.int32).reshape(WIDE_REPL, NARROW_REPL, ROUNDS, KMAX)


def draw_block_counts(key, part):
    total = WIDE_REPL * NARROW_REPL * ROUNDS
    first, second, third = jax.random.split(jax.random.fold_in(key, 7), 3)
    base = jax.random.randint(first, (total,), 1, KMAX // 2 + 1)
    busy = jax.random.randint(second, (total,), 0, 8) == 0
    base = jnp.where(busy, KMAX, base)
    chosen = jax.random.randint(third, (), 0, total)
    base = base.at[chosen].set(KMAX)
    return base.astype(jnp.int32).reshape(WIDE_REPL, NARROW_REPL, ROUNDS)


def level_of(key, dims, pieces, least, high):
    level = 1.0
    for position, shards_of in pieces:
        heights = jax.random.uniform(jax.random.fold_in(jax.random.fold_in(key, 6), position), (shards_of,), jnp.float32, least / len(pieces), high / len(pieces))
        level = level * jnp.repeat(jnp.exp(heights), dims[position] // shards_of).reshape((-1,) + (1,) * (len(dims) - 1 - position))
    return level


def bell_draw(key, extent, scale, bound, cuts=(), kind=jnp.bfloat16):
    array = scale * jax.random.normal(key, extent, jnp.float32)
    if cuts:
        array = array * level_of(key, extent, cuts, -0.22, 0.18)
    return jnp.clip(array, -bound, bound).astype(kind)


def setup_inputs(seed: int = 0) -> dict:
    key_of = jax.random.split(jax.random.key(seed), 8)
    params = bell_draw(key_of[0], (WIDE_REPL, NARROW_REPL, D, COLS), 1.0, 6.0, ((0, 64), (1, 4)), jnp.float32)
    public = bell_draw(key_of[1], (WIDE_REPL, NARROW_REPL, D, COLS), 1.0, 6.0, ((0, 64), (1, 4)), jnp.float32)
    mixed = bell_draw(key_of[2], (WIDE_REPL, NARROW_REPL, D, COLS), 1.0, 6.0, ((0, 64), (1, 4)), jnp.float32)
    inputs = bell_draw(key_of[3], (WIDE_REPL, NARROW_REPL, TOK_DEV, D), 1.0, 6.0, ((0, 64), (1, 4)))
    cotangent = bell_draw(key_of[4], (WIDE_REPL, NARROW_REPL, TOK_DEV, COLS), (4.0 / TOK_DEV ** 0.5), 1.5, ((0, 64), (1, 4)))
    block_ids = draw_block_ids(jax.random.fold_in(key_of[7], 71), 0)
    block_counts = draw_block_counts(jax.random.fold_in(key_of[7], 71), 0)
    return dict(params=params, public=public, mixed=mixed, inputs=inputs, cotangent=cotangent, block_ids=block_ids, block_counts=block_counts)


LEARN_RATE = 0.05
NEIGHBOUR_WEIGHT = 0.2
CONSENSUS = 0.4


def to_blocks(matrix):
    leading = matrix.shape[:-2]
    row_tiles = D // TILE
    col_tiles = COLS // TILE
    shaped = matrix.reshape(leading + (row_tiles, TILE, col_tiles, TILE))
    shaped = jnp.swapaxes(shaped, -3, -2)
    return shaped.reshape(leading + (row_tiles * col_tiles, TILE, TILE))


def from_blocks(blocks):
    leading = blocks.shape[:-3]
    row_tiles = D // TILE
    col_tiles = COLS // TILE
    shaped = blocks.reshape(leading + (row_tiles, col_tiles, TILE, TILE))
    shaped = jnp.swapaxes(shaped, -3, -2)
    return shaped.reshape(leading + (D, COLS))


def pick_one(current, public, listed):
    return current[listed] - public[listed]


def add_one(blocks, listed, values):
    return blocks.at[listed].add(values)


pick_all = jax.vmap(jax.vmap(pick_one))
add_all = jax.vmap(jax.vmap(add_one))


def reference(params, public, mixed, inputs, cotangent, block_ids, block_counts):
    gradient = jnp.einsum("abtd,abtc->abdc", inputs.astype(jnp.float32), cotangent.astype(jnp.float32))
    current = to_blocks(params - LEARN_RATE * gradient)
    public_blocks = to_blocks(public)
    mixed_blocks = to_blocks(mixed)
    slot_index = jnp.arange(KMAX, dtype=jnp.int32)
    for round_index in range(ROUNDS):
        listed = block_ids[:, :, round_index, :]
        in_use = slot_index[None, None, :] < block_counts[:, :, round_index, None]
        packed = jnp.where(in_use[..., None, None], pick_all(current, public_blocks, listed), 0.0)
        public_blocks = add_all(public_blocks, listed, packed)
        mixed_blocks = add_all(mixed_blocks, listed, NEIGHBOUR_WEIGHT * packed)
        for axis_num in (0, 1):
            for offset in (1, -1):
                moved = jnp.roll(packed, offset, axis=axis_num)
                moved_ids = jnp.roll(listed, offset, axis=axis_num)
                mixed_blocks = add_all(mixed_blocks, moved_ids, NEIGHBOUR_WEIGHT * moved)
        current = current + CONSENSUS * (mixed_blocks - public_blocks)
    return from_blocks(current), from_blocks(public_blocks), from_blocks(mixed_blocks)
```

```python
import functools

import jax
import jax.numpy as jnp
from jax import lax
from jax.experimental import pallas as pl
from jax.experimental.pallas import tpu as pltpu
from jax.sharding import PartitionSpec as P

D = 1024
COLS = 512
TILE = 128
KMAX = 8
TOKENS = 256
COL_TILES = COLS // TILE
BLOCKS = (D // TILE) * COL_TILES

LEARN_RATE = 0.05
NEIGHBOUR_WEIGHT = 0.2
CONSENSUS = 0.4

PIECES = 2
ROWS = TILE // PIECES
HEADER = 8


ANY = pl.BlockSpec(memory_space=pl.ANY)
SMEM = pl.BlockSpec(memory_space=pltpu.SMEM)
VMEM = pl.BlockSpec(memory_space=pltpu.VMEM)


def payload_rows(piece):
    return KMAX * ROWS + (HEADER if piece == 0 else 0)


def swaps(wide, narrow):
    def flat(w, n):
        return (w % wide) * narrow + n % narrow

    def exchange(edges):
        return [pair for a, b in edges for pair in ((a, b), (b, a))]

    every = [(w, n) for w in range(wide) for n in range(narrow)]
    return tuple(
        exchange(edges)
        for edges in (
            [(flat(w, n), flat(w + 1, n)) for w, n in every if w % 2 == 0],
            [(flat(w, n), flat(w, n + 1)) for w, n in every if n % 2 == 0],
            [(flat(w, n), flat(w, n + 1)) for w, n in every if n % 2 == 1],
            [(flat(w, n), flat(w + 1, n)) for w, n in every if w % 2 == 1],
        )
    )


def corner(tile):
    row = pl.multiple_of((tile // COL_TILES) * TILE, TILE)
    col = pl.multiple_of((tile % COL_TILES) * TILE, TILE)
    return row, col


def product(a, b):
    return lax.dot_general(a, b, (((0,), (0,)), ((), ())), preferred_element_type=jnp.float32)


def pack_first_kernel(
    ids, counts, params, public, inputs, cotangent, *refs
):
    outs = refs[:PIECES]
    a_buf, b_buf, p_buf, q_buf, ab_sem, pq_sem = refs[PIECES:]
    copies = [
        pltpu.make_async_copy(inputs, a_buf, ab_sem.at[0]),
        pltpu.make_async_copy(cotangent, b_buf, ab_sem.at[1]),
    ]
    for copy in copies:
        copy.start()
    windows = []
    for slot in range(KMAX):
        row, col = corner(ids[0, slot])
        window = (pl.ds(row, TILE), pl.ds(col, TILE))
        pair = (
            pltpu.make_async_copy(params.at[window], p_buf.at[slot], pq_sem.at[0, slot]),
            pltpu.make_async_copy(public.at[window], q_buf.at[slot], pq_sem.at[1, slot]),
        )
        pair[0].start()
        pair[1].start()
        windows.append((row, col, pair))
    lane = lax.broadcasted_iota(jnp.int32, (HEADER, TILE), 1)
    header = jnp.zeros((HEADER, TILE), jnp.float32)
    for round_index in range(2):
        for slot in range(KMAX):
            number = ids[round_index, slot].astype(jnp.float32)
            header = jnp.where(lane == round_index * KMAX + slot, number, header)
    outs[0][pl.ds(KMAX * ROWS, HEADER), :] = header
    for copy in copies:
        copy.wait()
    for slot in range(KMAX):
        row, col, pair = windows[slot]
        gradient = product(a_buf[:, pl.ds(row, TILE)], b_buf[:, pl.ds(col, TILE)])
        pair[0].wait()
        pair[1].wait()
        current = p_buf[slot] - LEARN_RATE * gradient
        packed = jnp.where(slot < counts[0], current - q_buf[slot], 0.0)
        for piece in range(PIECES):
            outs[piece][pl.ds(slot * ROWS, ROWS), :] = packed[piece * ROWS : (piece + 1) * ROWS]


def pack_first(ids, counts, params, public, inputs, cotangent):
    return pl.pallas_call(
        pack_first_kernel,
        name="pack_first",
        out_shape=[jax.ShapeDtypeStruct((payload_rows(h), TILE), jnp.float32) for h in range(PIECES)],
        in_specs=[SMEM, SMEM, ANY, ANY, ANY, ANY],
        out_specs=[VMEM] * PIECES,
        scratch_shapes=[
            pltpu.VMEM((TOKENS, D), jnp.bfloat16),
            pltpu.VMEM((TOKENS, COLS), jnp.bfloat16),
            pltpu.VMEM((KMAX, TILE, TILE), jnp.float32),
            pltpu.VMEM((KMAX, TILE, TILE), jnp.float32),
            pltpu.SemaphoreType.DMA((2,)),
            pltpu.SemaphoreType.DMA((2, KMAX)),
        ],
        cost_estimate=pl.CostEstimate(flops=2 * KMAX * TILE * TILE * TOKENS, bytes_accessed=3 << 20, transcendentals=0),
    )(ids, counts, params, public, inputs, cotangent)


def fill_own(table, ids, counts, round_index):
    for tile in range(BLOCKS):
        table[tile] = jnp.int32(-1)
    for slot in range(KMAX):

        @pl.when(slot < counts[round_index])
        def _():
            table[ids[round_index, slot]] = jnp.int32(slot)


def fill_tables(table, headers, round_index):
    for direction, header in enumerate(headers):
        base = direction * BLOCKS
        for tile in range(BLOCKS):
            table[base + tile] = jnp.int32(-1)
        for slot in range(KMAX):
            number = header[0, round_index * KMAX + slot].astype(jnp.int32)
            table[base + number] = jnp.int32(slot)


def arrivals(table, tile, refs):
    total = None
    for direction, ref in enumerate(refs):
        slot = table[direction * BLOCKS + tile]
        start = pl.multiple_of(jnp.maximum(slot, 0) * ROWS, ROWS)
        part = jnp.where(slot >= 0, ref[pl.ds(start, ROWS), :], 0.0)
        total = part if total is None else total + part
    return total


def first_step_kernel(ids, counts, params, public, mixed, inputs, cotangent, current_out, public_out, mixed_out, table):
    step = pl.program_id(0)

    @pl.when(step == 0)
    def _():
        fill_own(table, ids, counts, 0)

    current = params[...] - LEARN_RATE * product(inputs[...], cotangent[...])
    current_out[...] = current
    for j in range(COL_TILES):
        cols = slice(j * TILE, (j + 1) * TILE)
        used = table[step * COL_TILES + j] >= 0
        known = public[:, cols]
        packed = jnp.where(used, current[:, cols] - known, 0.0)
        public_out[:, cols] = known + packed
        mixed_out[:, cols] = mixed[:, cols] + NEIGHBOUR_WEIGHT * packed


def first_step(ids, counts, params, public, mixed, inputs, cotangent):
    rows = pl.BlockSpec((TILE, COLS), lambda i: (i, 0))
    whole = jax.ShapeDtypeStruct((D, COLS), jnp.float32)
    return pl.pallas_call(
        first_step_kernel,
        name="first_step",
        grid=(D // TILE,),
        out_shape=[whole] * 3,
        in_specs=[
            SMEM,
            SMEM,
            rows,
            rows,
            rows,
            pl.BlockSpec((TOKENS, TILE), lambda i: (0, i)),
            pl.BlockSpec((TOKENS, COLS), lambda i: (0, 0)),
        ],
        out_specs=[rows] * 3,
        scratch_shapes=[pltpu.SMEM((BLOCKS,), jnp.int32)],
        cost_estimate=pl.CostEstimate(flops=2 * D * COLS * TOKENS, bytes_accessed=13 << 20, transcendentals=0),
    )(ids, counts, params, public, mixed, inputs, cotangent)


def pack_second_kernel(piece, ids, counts, h0, h1, h2, h3, a0, a1, a2, a3, current, public, mixed, out, c_buf, p_buf, m_buf, table, sem):
    pending = []
    for slot in range(KMAX):
        row, col = corner(ids[1, slot])
        window = (pl.ds(pl.multiple_of(row + piece * ROWS, ROWS), ROWS), pl.ds(col, TILE))
        trio = [
            pltpu.make_async_copy(source.at[window], target.at[slot], sem.at[k, slot])
            for k, (source, target) in enumerate(((current, c_buf), (public, p_buf), (mixed, m_buf)))
        ]
        for copy in trio:
            copy.start()
        pending.append(trio)
    fill_tables(table, (h0, h1, h2, h3), 0)
    for slot in range(KMAX):
        total = arrivals(table, ids[1, slot], (a0, a1, a2, a3))
        for copy in pending[slot]:
            copy.wait()
        known = p_buf[slot]
        blend = m_buf[slot] + NEIGHBOUR_WEIGHT * total
        moved = c_buf[slot] + CONSENSUS * (blend - known)
        out[pl.ds(slot * ROWS, ROWS), :] = jnp.where(slot < counts[1], moved - known, 0.0)


def header_spec():
    place = KMAX * ROWS // HEADER
    return pl.BlockSpec((HEADER, TILE), lambda i: (place, 0), memory_space=pltpu.SMEM)


def pack_second(piece, ids, counts, heads, arrived, current, public, mixed):
    return pl.pallas_call(
        functools.partial(pack_second_kernel, piece),
        name=f"pack_second_{piece}",
        grid=(1,),
        out_shape=jax.ShapeDtypeStruct((KMAX * ROWS, TILE), jnp.float32),
        in_specs=[SMEM, SMEM] + [header_spec()] * 4 + [VMEM] * 4 + [ANY] * 3,
        out_specs=VMEM,
        scratch_shapes=[pltpu.VMEM((KMAX, ROWS, TILE), jnp.float32)] * 3
        + [pltpu.SMEM((4 * BLOCKS,), jnp.int32), pltpu.SemaphoreType.DMA((3, KMAX))],
        cost_estimate=pl.CostEstimate(flops=KMAX * ROWS * TILE * 12, bytes_accessed=(4 << 20) // PIECES, transcendentals=0),
    )(ids, counts, *heads, *arrived, current, public, mixed)


def second_step_kernel(ids, counts, h0, h1, h2, h3, *refs):
    came = refs[: 4 * PIECES]
    current, public, mixed, current_out, public_out, mixed_out, table, own = refs[4 * PIECES :]
    step = pl.program_id(0)

    @pl.when(step == 0)
    def _():
        fill_tables(table, (h0, h1, h2, h3), 0)
        fill_own(own, ids, counts, 1)

    for j in range(COL_TILES):
        cols = slice(j * TILE, (j + 1) * TILE)
        tile = step * COL_TILES + j
        used = own[tile] >= 0
        for piece in range(PIECES):
            rows = slice(piece * ROWS, (piece + 1) * ROWS)
            total = arrivals(table, tile, came[4 * piece : 4 * piece + 4])
            known = public[rows, cols]
            blend = mixed[rows, cols] + NEIGHBOUR_WEIGHT * total
            moved = current[rows, cols] + CONSENSUS * (blend - known)
            packed = jnp.where(used, moved - known, 0.0)
            known = known + packed
            blend = blend + NEIGHBOUR_WEIGHT * packed
            public_out[rows, cols] = known
            mixed_out[rows, cols] = blend
            current_out[rows, cols] = moved + CONSENSUS * (blend - known)


def second_step(ids, counts, heads, arrived, current, public, mixed):
    rows = pl.BlockSpec((TILE, COLS), lambda i: (i, 0))
    whole = jax.ShapeDtypeStruct((D, COLS), jnp.float32)
    return pl.pallas_call(
        second_step_kernel,
        name="second_step",
        grid=(D // TILE,),
        out_shape=[whole] * 3,
        in_specs=[SMEM, SMEM] + [header_spec()] * 4 + [VMEM] * (4 * PIECES) + [rows] * 3,
        out_specs=[rows] * 3,
        scratch_shapes=[pltpu.SMEM((4 * BLOCKS,), jnp.int32), pltpu.SMEM((BLOCKS,), jnp.int32)],
        cost_estimate=pl.CostEstimate(flops=D * COLS * 16, bytes_accessed=14 << 20, transcendentals=0),
    )(ids, counts, *heads, *arrived, current, public, mixed)


def finish_kernel(h0, h1, h2, h3, a0, a1, a2, a3, current, mixed, current_out, mixed_out, table):
    step = pl.program_id(0)

    @pl.when(step == 0)
    def _():
        fill_tables(table, (h0, h1, h2, h3), 1)

    for j in range(COL_TILES):
        cols = slice(j * TILE, (j + 1) * TILE)
        total = arrivals(table, step * COL_TILES + j, (a0, a1, a2, a3))
        mixed_out[:, cols] = mixed[:, cols] + NEIGHBOUR_WEIGHT * total
        current_out[:, cols] = current[:, cols] + (CONSENSUS * NEIGHBOUR_WEIGHT) * total


def finish(piece, heads, arrived, current, mixed):
    rows = pl.BlockSpec((ROWS, COLS), lambda i: (i * PIECES + piece, 0))
    whole = jax.ShapeDtypeStruct((D, COLS), jnp.float32)
    return pl.pallas_call(
        finish_kernel,
        name=f"finish_{piece}",
        grid=(D // TILE,),
        out_shape=[whole] * 2,
        in_specs=[header_spec()] * 4 + [VMEM] * 4 + [rows] * 2,
        out_specs=[rows] * 2,
        scratch_shapes=[pltpu.SMEM((4 * BLOCKS,), jnp.int32)],
        input_output_aliases={8: 0, 9: 1},
        cost_estimate=pl.CostEstimate(flops=D * COLS * 8 // PIECES, bytes_accessed=(10 << 20) // PIECES, transcendentals=0),
    )(*heads, *arrived, current, mixed)


def on_device(exchanges, params, public, mixed, inputs, cotangent, block_ids, block_counts):
    params, public, mixed = params[0, 0], public[0, 0], mixed[0, 0]
    inputs, cotangent = inputs[0, 0], cotangent[0, 0]
    ids, counts = block_ids[0, 0], block_counts[0, 0]

    def send(value):
        return [lax.ppermute(value, ("wide", "narrow"), pairs) for pairs in exchanges]

    outgoing = pack_first(ids, counts, params, public, inputs, cotangent)
    came = [send(value) for value in outgoing]
    heads = came[0]
    current, public, mixed = first_step(ids, counts, params, public, mixed, inputs, cotangent)
    later = [
        send(pack_second(piece, ids, counts, heads, came[piece], current, public, mixed))
        for piece in range(PIECES)
    ]
    current, public, mixed = second_step(
        ids, counts, heads, [value for piece in came for value in piece], current, public, mixed
    )
    for piece in range(PIECES):
        current, mixed = finish(piece, heads, later[piece], current, mixed)
    return tuple(value.reshape(1, 1, D, COLS) for value in (current, public, mixed))


def solution(mesh):
    exchanges = swaps(mesh.shape["wide"], mesh.shape["narrow"])
    array = P("wide", "narrow", None, None)
    return jax.shard_map(
        functools.partial(on_device, exchanges),
        mesh=mesh,
        in_specs=(array,) * 6 + (P("wide", "narrow", None),),
        out_specs=(array,) * 3,
        check_vma=False,
    )
```

```python
import functools

import jax
import jax.numpy as jnp
from jax import lax
from jax.experimental import pallas as pl
from jax.experimental.pallas import tpu as pltpu
from jax.sharding import PartitionSpec as P

D = 1024
COLS = 512
TILE = 128
KMAX = 8
TOKENS = 256
ROW_TILES = D // TILE
COL_TILES = COLS // TILE
BLOCKS = ROW_TILES * COL_TILES

LEARN_RATE = 0.05
NEIGHBOUR_WEIGHT = 0.2
CONSENSUS = 0.4

PIECES = 2
ROWS = TILE // PIECES
HEADER = 8
HEADER_ROW = KMAX * ROWS


ANY = pl.BlockSpec(memory_space=pl.ANY)
SMEM = pl.BlockSpec(memory_space=pltpu.SMEM)
VMEM = pl.BlockSpec(memory_space=pltpu.VMEM)


PARAMS = pltpu.CompilerParams(vmem_limit_bytes=12 << 20)


def near(value):
    return pltpu.with_memory_space_constraint(value, pltpu.VMEM)


def far(value):
    return pltpu.with_memory_space_constraint(value, pltpu.HBM)


def payload(piece):
    return pltpu.VMEM((HEADER_ROW + (HEADER if piece == 0 else 0), TILE), jnp.float32)


def swaps(wide, narrow):
    def flat(w, n):
        return (w % wide) * narrow + n % narrow

    def exchange(edges):
        return [pair for a, b in edges for pair in ((a, b), (b, a))]

    every = [(w, n) for w in range(wide) for n in range(narrow)]
    return tuple(
        exchange(edges)
        for edges in (
            [(flat(w, n), flat(w + 1, n)) for w, n in every if w % 2 == 0],
            [(flat(w, n), flat(w, n + 1)) for w, n in every if n % 2 == 0],
            [(flat(w, n), flat(w, n + 1)) for w, n in every if n % 2 == 1],
            [(flat(w, n), flat(w + 1, n)) for w, n in every if w % 2 == 1],
        )
    )


def corner(tile):
    row = pl.multiple_of((tile // COL_TILES) * TILE, TILE)
    col = pl.multiple_of((tile % COL_TILES) * TILE, TILE)
    return row, col


def product(a, b):
    return lax.dot_general(a, b, (((0,), (0,)), ((), ())), preferred_element_type=jnp.float32)


def pack_first_kernel(ids, counts, params, public, inputs, cotangent, out, a_buf, b_buf, p_buf, q_buf, ab_sem, pq_sem):
    pending = []
    for slot in range(KMAX):
        row, col = corner(ids[0, slot])
        window = (pl.ds(row, ROWS), pl.ds(col, TILE))
        pair = (
            pltpu.make_async_copy(params.at[window], p_buf.at[slot], pq_sem.at[0, slot]),
            pltpu.make_async_copy(public.at[window], q_buf.at[slot], pq_sem.at[1, slot]),
        )
        pending.append((row, col, pair))
        if slot == 0:
            whole = (
                pltpu.make_async_copy(inputs, a_buf, ab_sem.at[0]),
                pltpu.make_async_copy(cotangent, b_buf, ab_sem.at[1]),
            )
            whole[0].start()
            whole[1].start()
        pair[0].start()
        pair[1].start()
    lane = lax.broadcasted_iota(jnp.int32, (HEADER, TILE), 1)
    header = jnp.zeros((HEADER, TILE), jnp.float32)
    for round_index in range(2):
        for slot in range(KMAX):
            number = ids[round_index, slot].astype(jnp.float32)
            header = jnp.where(lane == round_index * KMAX + slot, number, header)
    out[pl.ds(HEADER_ROW, HEADER), :] = header
    whole[0].wait()
    whole[1].wait()
    for slot in range(KMAX):
        row, col, pair = pending[slot]
        gradient = product(a_buf[:, pl.ds(row, TILE)], b_buf[:, pl.ds(col, TILE)])[:ROWS]
        pair[0].wait()
        pair[1].wait()
        current = p_buf[slot] - LEARN_RATE * gradient
        out[pl.ds(slot * ROWS, ROWS), :] = jnp.where(slot < counts[0], current - q_buf[slot], 0.0)


def pack_first(ids, counts, params, public, inputs, cotangent):
    return pl.pallas_call(
        pack_first_kernel,
        name="pack_first",
        out_shape=payload(0),
        in_specs=[SMEM, SMEM, ANY, ANY, ANY, ANY],
        out_specs=VMEM,
        scratch_shapes=[
            pltpu.VMEM((TOKENS, D), jnp.bfloat16),
            pltpu.VMEM((TOKENS, COLS), jnp.bfloat16),
            pltpu.VMEM((KMAX, ROWS, TILE), jnp.float32),
            pltpu.VMEM((KMAX, ROWS, TILE), jnp.float32),
            pltpu.SemaphoreType.DMA((2,)),
            pltpu.SemaphoreType.DMA((2, KMAX)),
        ],
        compiler_params=PARAMS,
        cost_estimate=pl.CostEstimate(flops=2 * KMAX * TILE * TILE * TOKENS, bytes_accessed=3 << 20, transcendentals=0),
    )(*map(far, (ids, counts, params, public, inputs, cotangent)))


def fill_own(table, ids, counts, round_index):
    for tile in range(BLOCKS):
        table[tile] = jnp.int32(-1)
    for slot in range(KMAX):

        @pl.when(slot < counts[round_index])
        def _():
            table[ids[round_index, slot]] = jnp.int32(slot)


def first_step_kernel(
    ids, counts, params, public, mixed, inputs, cotangent, current_out, public_out, mixed_out, packed_out, a_buf, b_buf, table, ab_sem, sem
):
    whole = (
        pltpu.make_async_copy(inputs, a_buf, ab_sem.at[0]),
        pltpu.make_async_copy(cotangent, b_buf, ab_sem.at[1]),
    )
    whole[0].start()
    whole[1].start()
    pending = []
    for i in range(ROW_TILES):
        window = pl.ds(i * TILE, TILE)
        trio = [
            pltpu.make_async_copy(source.at[window, :], target.at[window, :], sem.at[k, i])
            for k, (source, target) in enumerate(((params, current_out), (public, public_out), (mixed, mixed_out)))
        ]
        for copy in trio:
            copy.start()
        pending.append(trio)
    fill_own(table, ids, counts, 0)
    packed_out[...] = jnp.zeros_like(packed_out)
    whole[0].wait()
    whole[1].wait()
    for i in range(ROW_TILES):
        rows = slice(i * TILE, (i + 1) * TILE)
        gradient = product(a_buf[:, rows], b_buf[...])
        for copy in pending[i]:
            copy.wait()
        current_out[rows, :] = current_out[rows, :] - LEARN_RATE * gradient
        for j in range(COL_TILES):
            cols = slice(j * TILE, (j + 1) * TILE)
            slot = table[i * COL_TILES + j]

            @pl.when(slot >= 0)
            def _():
                known = public_out[rows, cols]
                packed = current_out[rows, cols] - known
                public_out[rows, cols] = known + packed
                mixed_out[rows, cols] = mixed_out[rows, cols] + NEIGHBOUR_WEIGHT * packed
                packed_out[pl.ds(pl.multiple_of(slot * ROWS, ROWS), ROWS), :] = packed[ROWS:]


def first_step(ids, counts, params, public, mixed, inputs, cotangent):
    return pl.pallas_call(
        first_step_kernel,
        name="first_step",
        out_shape=[pltpu.VMEM((D, COLS), jnp.float32)] * 3 + [payload(1)],
        in_specs=[SMEM, SMEM] + [ANY] * 5,
        out_specs=[VMEM] * 4,
        scratch_shapes=[
            pltpu.VMEM((TOKENS, D), jnp.bfloat16),
            pltpu.VMEM((TOKENS, COLS), jnp.bfloat16),
            pltpu.SMEM((BLOCKS,), jnp.int32),
            pltpu.SemaphoreType.DMA((2,)),
            pltpu.SemaphoreType.DMA((3, ROW_TILES)),
        ],
        compiler_params=PARAMS,
        cost_estimate=pl.CostEstimate(flops=2 * D * COLS * TOKENS, bytes_accessed=13 << 20, transcendentals=0),
    )(*map(far, (ids, counts, params, public, mixed, inputs, cotangent)))


def arrivals(table, base, tile, refs):
    total = None
    for direction, ref in enumerate(refs):
        slot = table[base + direction * BLOCKS + tile]
        start = pl.multiple_of(jnp.maximum(slot, 0) * ROWS, ROWS)
        part = jnp.where(slot >= 0, ref[pl.ds(start, ROWS), :], 0.0)
        total = part if total is None else total + part
    return total


def fill_tables(table, numbers):
    for place in range(2 * 4 * BLOCKS):
        table[place] = jnp.int32(-1)
    for round_index in range(2):
        for direction in range(4):
            for slot in range(KMAX):
                number = numbers[direction, 0, round_index * KMAX + slot].astype(jnp.int32)
                table[(round_index * 4 + direction) * BLOCKS + number] = jnp.int32(slot)


def pack_second_body(piece, ids, counts, table, came, current, public, mixed, out):
    for slot in range(KMAX):
        tile = ids[1, slot]
        row, col = corner(tile)
        window = (pl.ds(pl.multiple_of(row + piece * ROWS, ROWS), ROWS), pl.ds(col, TILE))
        total = arrivals(table, 0, tile, came)
        known = public[window]
        blend = mixed[window] + NEIGHBOUR_WEIGHT * total
        moved = current[window] + CONSENSUS * (blend - known)
        out[pl.ds(slot * ROWS, ROWS), :] = jnp.where(slot < counts[1], moved - known, 0.0)


def pack_second_first_kernel(ids, counts, a0, a1, a2, a3, current, public, mixed, out, table_out, numbers, sem):
    came = (a0, a1, a2, a3)
    copies = [
        pltpu.make_async_copy(ref.at[pl.ds(HEADER_ROW, HEADER), :], numbers.at[direction], sem.at[direction])
        for direction, ref in enumerate(came)
    ]
    for copy in copies:
        copy.start()
    for copy in copies:
        copy.wait()
    fill_tables(table_out, numbers)
    pack_second_body(0, ids, counts, table_out, came, current, public, mixed, out)


def pack_second_last_kernel(ids, counts, table, a0, a1, a2, a3, current, public, mixed, out):
    pack_second_body(1, ids, counts, table, (a0, a1, a2, a3), current, public, mixed, out)


PACK_COST = pl.CostEstimate(flops=KMAX * ROWS * TILE * 12, bytes_accessed=2 << 20, transcendentals=0)


def pack_second_first(ids, counts, came, state):
    return pl.pallas_call(
        pack_second_first_kernel,
        name="pack_second_first",
        out_shape=[pltpu.VMEM((HEADER_ROW, TILE), jnp.float32), jax.ShapeDtypeStruct((2 * 4 * BLOCKS,), jnp.int32)],
        in_specs=[SMEM, SMEM] + [VMEM] * 7,
        out_specs=[VMEM, SMEM],
        scratch_shapes=[pltpu.SMEM((4, HEADER, TILE), jnp.float32), pltpu.SemaphoreType.DMA((4,))],
        compiler_params=PARAMS,
        cost_estimate=PACK_COST,
    )(far(ids), far(counts), *map(near, came), *map(near, state))


def pack_second_last(ids, counts, table, came, state):
    return pl.pallas_call(
        pack_second_last_kernel,
        name="pack_second_last",
        out_shape=pltpu.VMEM((HEADER_ROW, TILE), jnp.float32),
        in_specs=[SMEM] * 3 + [VMEM] * 7,
        out_specs=VMEM,
        compiler_params=PARAMS,
        cost_estimate=PACK_COST,
    )(far(ids), far(counts), table, *map(near, came), *map(near, state))


def second_step_kernel(ids, counts, table, *refs):
    came = refs[: 4 * PIECES]
    current, public, mixed, current_out, public_out, mixed_out, p_buf, own, sem = refs[4 * PIECES :]
    fill_own(own, ids, counts, 1)
    copies = []
    for i in range(ROW_TILES):
        for j in range(COL_TILES):
            cols = slice(j * TILE, (j + 1) * TILE)
            tile = i * COL_TILES + j
            used = own[tile] >= 0
            for piece in range(PIECES):
                rows = slice(i * TILE + piece * ROWS, i * TILE + (piece + 1) * ROWS)
                total = arrivals(table, 0, tile, came[4 * piece : 4 * piece + 4])
                known = public[rows, cols]
                blend = mixed[rows, cols] + NEIGHBOUR_WEIGHT * total
                moved = current[rows, cols] + CONSENSUS * (blend - known)
                packed = jnp.where(used, moved - known, 0.0)
                known = known + packed
                blend = blend + NEIGHBOUR_WEIGHT * packed
                p_buf[rows, cols] = known
                mixed_out[rows, cols] = blend
                current_out[rows, cols] = moved + CONSENSUS * (blend - known)
        window = pl.ds(i * TILE, TILE)
        copy = pltpu.make_async_copy(p_buf.at[window, :], public_out.at[window, :], sem.at[i])
        copy.start()
        copies.append(copy)
    for copy in copies:
        copy.wait()


def second_step(ids, counts, table, came, state):
    local = pltpu.VMEM((D, COLS), jnp.float32)
    return pl.pallas_call(
        second_step_kernel,
        name="second_step",
        out_shape=[local, pltpu.HBM((D, COLS), jnp.float32), local],
        in_specs=[SMEM] * 3 + [VMEM] * (4 * PIECES + 3),
        out_specs=[VMEM, ANY, VMEM],
        scratch_shapes=[
            pltpu.VMEM((D, COLS), jnp.float32),
            pltpu.SMEM((BLOCKS,), jnp.int32),
            pltpu.SemaphoreType.DMA((ROW_TILES,)),
        ],
        compiler_params=PARAMS,
        cost_estimate=pl.CostEstimate(flops=D * COLS * 16, bytes_accessed=14 << 20, transcendentals=0),
    )(far(ids), far(counts), table, *map(near, came), *map(near, state))


def finish_kernel(piece, table, a0, a1, a2, a3, current, mixed, *refs):
    current_out, mixed_out, c_buf, m_buf, sem = refs[-5:]
    copies = []
    for i in range(ROW_TILES):
        rows = slice(i * TILE + piece * ROWS, i * TILE + (piece + 1) * ROWS)
        local = slice(i * ROWS, (i + 1) * ROWS)
        for j in range(COL_TILES):
            cols = slice(j * TILE, (j + 1) * TILE)
            total = arrivals(table, 4 * BLOCKS, i * COL_TILES + j, (a0, a1, a2, a3))
            m_buf[local, cols] = mixed[rows, cols] + NEIGHBOUR_WEIGHT * total
            c_buf[local, cols] = current[rows, cols] + (CONSENSUS * NEIGHBOUR_WEIGHT) * total
        for k, (source, target) in enumerate(((c_buf, current_out), (m_buf, mixed_out))):
            copy = pltpu.make_async_copy(
                source.at[pl.ds(i * ROWS, ROWS), :], target.at[pl.ds(i * TILE + piece * ROWS, ROWS), :], sem.at[k, i]
            )
            copy.start()
            copies.append(copy)
    for copy in copies:
        copy.wait()


def finish(piece, table, came, current, mixed, outs):
    return pl.pallas_call(
        functools.partial(finish_kernel, piece),
        name=f"finish_{piece}",
        out_shape=[pltpu.HBM((D, COLS), jnp.float32)] * 2,
        in_specs=[SMEM] + [VMEM] * 6 + [ANY] * len(outs),
        out_specs=[ANY] * 2,
        scratch_shapes=[
            pltpu.VMEM((ROW_TILES * ROWS, COLS), jnp.float32),
            pltpu.VMEM((ROW_TILES * ROWS, COLS), jnp.float32),
            pltpu.SemaphoreType.DMA((2, ROW_TILES)),
        ],
        input_output_aliases={7: 0, 8: 1} if outs else {},
        compiler_params=PARAMS,
        cost_estimate=pl.CostEstimate(flops=D * COLS * 4, bytes_accessed=5 << 20, transcendentals=0),
    )(table, *map(near, came), near(current), near(mixed), *outs)


def on_device(exchanges, params, public, mixed, inputs, cotangent, block_ids, block_counts):
    params, public, mixed = params[0, 0], public[0, 0], mixed[0, 0]
    inputs, cotangent = inputs[0, 0], cotangent[0, 0]
    ids, counts = block_ids[0, 0], block_counts[0, 0]

    def send(value):
        return [lax.ppermute(value, ("wide", "narrow"), pairs) for pairs in exchanges]

    came_0 = send(pack_first(ids, counts, params, public, inputs, cotangent))
    *state, packed = first_step(ids, counts, params, public, mixed, inputs, cotangent)
    came_1 = send(packed)
    packed, table = pack_second_first(ids, counts, came_0, state)
    later_0 = send(packed)
    later_1 = send(pack_second_last(ids, counts, table, came_1, state))
    current, public, mixed = second_step(ids, counts, table, came_0 + came_1, state)
    outs = finish(0, table, later_0, current, mixed, ())
    current, mixed = finish(1, table, later_1, current, mixed, outs)
    return tuple(value.reshape(1, 1, D, COLS) for value in (current, public, mixed))


def solution(mesh):
    exchanges = swaps(mesh.shape["wide"], mesh.shape["narrow"])
    array = P("wide", "narrow", None, None)
    return jax.shard_map(
        functools.partial(on_device, exchanges),
        mesh=mesh,
        in_specs=(array,) * 6 + (P("wide", "narrow", None),),
        out_specs=(array,) * 3,
        check_vma=False,
    )
```
